256 devices in a mesh: blk: 16 (over z, core), segment: 2 (over y_hi), rep: 8 (over x, y_lo).
Axes of the slice: x: 4, y: 4 (y_hi: 2, y_lo: 2; y = y_hi * 2 + y_lo), z: 8, core: 2. Of those that a mesh axis runs over, the one named last changes fastest.
Arguments:
- features: bfloat16 [16384, 256], P('blk'), may hold values from -14 to 14
- tile_weight: bfloat16 [49152, 128, 128], P(('blk', 'segment', 'rep')), may hold values from -0.099609375 to 0.099609375
- tile_limit: int32 [49152, 128], P(('blk', 'segment', 'rep')), may hold values from 1 to 128
- tile_src: int32 [49152, 1], P(('blk', 'segment', 'rep')), may hold values from 0 to 15; in each aligned block of 192 rows (0 to 191, 192 to 383, ...) at most 24 rows name the same one
- tile_row: int32 [49152], P(('blk', 'segment', 'rep')), may hold values from 0 to 5
- tile_col: int32 [49152], P(('blk', 'segment', 'rep')), may hold values from 0 to 7
- gain_one: float32 [256], replicated, may hold values from 0.25 to 1.75
- up_one: bfloat16 [256, 1024], replicated, may hold values from -0.375 to 0.375
- down_one: bfloat16 [1024, 256], replicated, may hold values from -0.25 to 0.25
- gain_two: float32 [256], replicated, may hold values from 0.25 to 1.75
- gate_two: bfloat16 [256, 2048], P(None, ('segment', 'rep')), may hold values from -0.375 to 0.375
- up_two: bfloat16 [256, 2048], P(None, ('segment', 'rep')), may hold values from -0.375 to 0.375
- down_two: bfloat16 [256, 2048], P(None, ('segment', 'rep')), may hold values from -0.25 to 0.25
Outputs:
- readout: bfloat16 [196608, 256], P(('blk', 'segment', 'rep'))
The draws below stay inside these ranges and needn't reach their ends.
Inputs may be any that keep to these rules, and one draw needn't show every extreme that they name: `tile_src`: among the 192 tiles of one device at most 24 name the same partition, a bound that some block reaches.
All inputs are finite; a program needn't handle non-finite values.
Results may differ from the reference program's by a relative error of at most 0.0062.
Values may be sent and summed in bfloat16 or wider, within the bound.
No kernel may reach another device: no remote copies, remote signals or barrier semaphores. Data moves between devices by JAX's collectives and lax.ppermute only.
A program may use at most 128 MiB of HBM per device.

```python
import math
import jax
import jax.numpy as jnp
import numpy as np
from jax import lax

FEATURES = 256
HIDDEN_ONE = 1024
HIDDEN_TWO = 2048
TILE_SIZE = 128
SRC_BLOCK = 1024
DEST_DEV = 768
TILE_COUNT = 192
SLOT_CAP = 24
BLOCKS = 16
SOURCES = 16384
DEST_TOTAL = 196608
TILE_TOTAL = 49152


def draw_features(key, part):
    key_base = jax.random.fold_in(key, 11)
    key_rows = jax.random.fold_in(key, 12)
    key_cols = jax.random.fold_in(key, 13)
    normal_part = jax.random.normal(key_base, (SOURCES, FEATURES), jnp.float32)
    row_scale = jax.random.uniform(key_rows, (SOURCES, 1), jnp.float32, -0.6, 0.6)
    col_scale = jax.random.uniform(key_cols, (1, FEATURES), jnp.float32, -0.6, 0.6)
    values = normal_part * jnp.exp(row_scale + col_scale)
    return jnp.clip(values, -14.0, 14.0).astype(jnp.bfloat16)


def plant(array, key, smallest, high):
    longest = array.shape.index(max(array.shape))
    spots = []
    for shift in (0, 1):
        where = [jax.random.randint(jax.random.fold_in(key, axis), (), 0, length) for axis, length in enumerate(array.shape)]
        where[longest] = (where[longest] + shift) % array.shape[longest]
        spots.append(tuple(where))
    return array.at[spots[0]].set(smallest).at[spots[1]].set(high)


def steps_of(stream_key, extent, pieces, low, high):
    def one(dim, blocks):
        steps = jax.random.uniform(jax.random.fold_in(jax.random.fold_in(stream_key, 6), dim), (blocks,), jnp.float32, low / len(pieces), high / len(pieces))
        return jnp.repeat(jnp.exp(steps), extent[dim] // blocks).reshape((-1,) + (1,) * (len(extent) - dim - 1))

    factor_of = one(*pieces[0])
    for cut in pieces[1:]:
        factor_of = factor_of * one(*cut)
    return factor_of


def routed_block(rng, own, number, rows, amount, top, bound, skew):
    sequence = jax.random.permutation(rng, amount)
    crowded, usual = shares(amount, rows * top, bound, skew, True), shares(amount, rows * top, bound, skew, False)
    places = jnp.arange(amount)

    def named(tallies, rotation):
        used = int((tallies > 0).sum())
        fixed = max(1, used // 4)
        shifted = fixed + (places - fixed + rotation * (used - fixed)) % max(1, amount - fixed)
        return jnp.zeros((amount,), jnp.int32).at[sequence[jnp.where(places < fixed, places, shifted)]].set(jnp.asarray(tallies, jnp.int32))

    tallies = jnp.where(number % 4 == 0, named(crowded, number // 4), named(usual, number - number // 4 - 1))
    mixed = jax.random.permutation(jax.random.fold_in(own, 3), amount)
    donor, sink = mixed[0:amount // 2 * 2:2], mixed[1:amount // 2 * 2:2]
    room = jnp.minimum(tallies[donor] - 1, bound - tallies[sink]) // 2
    room = jnp.where((donor == sequence[0]) | (sink == sequence[0]) | (tallies[sink] == 0), 0, jnp.maximum(room, 0))
    shifted = jax.random.randint(jax.random.fold_in(own, 4), (amount // 2,), 0, 1 << 20) % (room + 1)
    tallies = tallies.at[donor].add(-shifted).at[sink].add(shifted)
    members = jnp.searchsorted(jnp.cumsum(tallies), jnp.arange(rows * top), side="right").astype(jnp.int32)
    grid = members.reshape(top, rows).T
    grid = grid[jax.random.permutation(jax.random.fold_in(own, 1), rows)]
    rotation = jax.random.randint(jax.random.fold_in(own, 2), (rows, 1), 0, top)
    return jnp.take_along_axis(grid, (jnp.arange(top)[None, :] + rotation) % top, axis=1)


def shares(count, total, most, lean, full):
    weights = [(1 << 20) // math.isqrt(standing ** lean) + 1 for standing in range(1, count + 1)]
    largest = most if full else min(most, max(-(-total // count), total * weights[0] // sum(weights)))
    least = 1 if total - largest >= count - 1 else 0
    counts, rest = [largest] + [least] * (count - 1), total - largest - least * (count - 1)
    while rest > 0:
        candidates = [i for i in range(1, count) if counts[i] < largest] or [i for i in range(1, count) if counts[i] < most]
        mass, left = sum([weights[i] for i in candidates]), rest
        for i in candidates:
            extra = min(most - counts[i], max(1, left * weights[i] // mass), rest)
            counts[i] = counts[i] + extra
            rest = rest - extra
    return np.array(counts)


def normal_values(own_key, shape, spread, bound, shards=(), held_as=jnp.bfloat16):
    values = spread * jax.random.normal(own_key, shape, jnp.float32)
    if shards:
        values = values * steps_of(own_key, shape, shards, -0.22, 0.18)
    return jnp.clip(values, -bound, bound).astype(held_as)


def setup_inputs(seed: int = 0) -> dict:
    arg_keys = jax.random.split(jax.random.key(seed), 14)
    features = draw_features(jax.random.fold_in(arg_keys[13], 71), 0)
    tile_weight = normal_values(arg_keys[1], (TILE_TOTAL, TILE_SIZE, TILE_SIZE), 0.018, 0.099609375, ((0, 256),))
    tile_limit = plant(jax.random.randint(arg_keys[2], (TILE_TOTAL, TILE_SIZE), 1, TILE_SIZE + 1), jax.random.fold_in(arg_keys[2], 1), 1, TILE_SIZE).astype(jnp.int32)
    tile_src_keys = jax.random.split(jax.random.fold_in(arg_keys[3], 1), TILE_TOTAL // TILE_COUNT)
    tile_src_turns = jax.random.permutation(jax.random.fold_in(arg_keys[3], 3), TILE_TOTAL // TILE_COUNT)
    tile_src = jax.vmap(lambda own, number: routed_block(jax.random.fold_in(arg_keys[3], 2), own, number, TILE_COUNT, BLOCKS, 1, SLOT_CAP, 2))(tile_src_keys, tile_src_turns).reshape((TILE_TOTAL, 1))
    tile_row = plant(jax.random.randint(arg_keys[4], (TILE_TOTAL,), 0, DEST_DEV // TILE_SIZE), jax.random.fold_in(arg_keys[4], 1), 0, (DEST_DEV // TILE_SIZE) - 1).astype(jnp.int32)
    tile_col = plant(jax.random.randint(arg_keys[5], (TILE_TOTAL,), 0, SRC_BLOCK // TILE_SIZE), jax.random.fold_in(arg_keys[5], 1), 0, (SRC_BLOCK // TILE_SIZE) - 1).astype(jnp.int32)
    gain_one = jnp.clip(1.0 + 0.15 * jax.random.normal(arg_keys[6], (FEATURES,), jnp.float32), 0.25, 1.75)
    up_one = normal_values(arg_keys[7], (FEATURES, HIDDEN_ONE), FEATURES ** -0.5, 0.375)
    down_one = normal_values(arg_keys[8], (HIDDEN_ONE, FEATURES), (HIDDEN_ONE // 2) ** -0.5, 0.25)
    gain_two = jnp.clip(1.0 + 0.15 * jax.random.normal(arg_keys[9], (FEATURES,), jnp.float32), 0.25, 1.75)
    gate_two = normal_values(arg_keys[10], (FEATURES, HIDDEN_TWO), FEATURES ** -0.5, 0.375, ((1, 16),))
    up_two = normal_values(arg_keys[11], (FEATURES, HIDDEN_TWO), FEATURES ** -0.5, 0.375, ((1, 16),))
    down_two = normal_values(arg_keys[12], (FEATURES, HIDDEN_TWO), (HIDDEN_TWO // 4) ** -0.5, 0.25, ((1, 16),))
    return {"features": features, "tile_weight": tile_weight, "tile_limit": tile_limit, "tile_src": tile_src, "tile_row": tile_row, "tile_col": tile_col, "gain_one": gain_one, "up_one": up_one, "down_one": down_one, "gain_two": gain_two, "gate_two": gate_two, "up_two": up_two, "down_two": down_two}


def rms_scaled(values, norm_gain):
    mean_square = lax.optimization_barrier(jnp.mean(values * values, axis=-1, keepdims=True))
    return values * lax.rsqrt(mean_square + 1e-06) * norm_gain.astype(jnp.float32)

def reference(features, tile_weight, tile_limit, tile_src, tile_row, tile_col, gain_one, up_one, down_one, gain_two, gate_two, up_two, down_two):
    device_count = TILE_TOTAL // TILE_COUNT
    row_tiles = DEST_DEV // TILE_SIZE
    col_tiles = SRC_BLOCK // TILE_SIZE
    tiles_all = features.reshape(-1, TILE_SIZE, FEATURES)
    columns = jnp.arange(TILE_SIZE, dtype=jnp.int32)
    row_ids = jnp.arange(row_tiles, dtype=jnp.int32)

    def one_device(carried, inputs):
        weight, row_limit, source_part, dest_tile, source_col = inputs
        masked = jnp.where(columns[None, None, :] < row_limit[:, :, None], weight, jnp.zeros((), weight.dtype))
        tile_index = (source_part * col_tiles + source_col).astype(jnp.int32)
        picked = tiles_all[tile_index]
        contrib = jnp.einsum('tij,tjf->tif', masked.astype(jnp.float32), picked.astype(jnp.float32))
        onehot = (dest_tile[:, None] == row_ids[None, :]).astype(jnp.float32)
        summed = jnp.einsum('tr,tif->rif', onehot, contrib, precision=lax.Precision.HIGHEST)
        aggregated = summed.reshape(DEST_DEV, FEATURES)
        normed_one = rms_scaled(aggregated, gain_one).astype(jnp.bfloat16)
        hidden_one = jnp.maximum(jnp.dot(normed_one, up_one, preferred_element_type=jnp.float32), 0.0).astype(jnp.bfloat16)
        section_one = aggregated + jnp.dot(hidden_one, down_one, preferred_element_type=jnp.float32)
        normed_two = rms_scaled(section_one, gain_two).astype(jnp.bfloat16)
        gate_value = jnp.dot(normed_two, gate_two, preferred_element_type=jnp.float32)
        up_value = jnp.dot(normed_two, up_two, preferred_element_type=jnp.float32)
        hidden_two = (jax.nn.silu(gate_value) * up_value).astype(jnp.bfloat16)
        branch_two = lax.dot_general(hidden_two, down_two, (((1,), (1,)), ((), ())), preferred_element_type=jnp.float32)
        return (carried, (section_one + branch_two).astype(jnp.bfloat16))
    inputs = (tile_weight.reshape(device_count, TILE_COUNT, TILE_SIZE, TILE_SIZE), tile_limit.reshape(device_count, TILE_COUNT, TILE_SIZE), tile_src.reshape(device_count, TILE_COUNT), tile_row.reshape(device_count, TILE_COUNT), tile_col.reshape(device_count, TILE_COUNT))
    unused, outputs = lax.scan(one_device, jnp.zeros((), jnp.float32), inputs)
    return outputs.reshape(DEST_TOTAL, FEATURES)
```

```python
import jax
import jax.numpy as jnp
from jax import lax
from jax.experimental import pallas as pl
from jax.experimental.pallas import tpu as pltpu
from jax.sharding import Mesh, PartitionSpec as P


FEATURES = 256
TILE = 128
SRC = 1024
DEST = 768
TILES = 192
ROWS = DEST // TILE
COLS = SRC // TILE
HIDDEN_ONE = 1024
SHARD = 384
HALF = SHARD // 2
RING = 8
PACK = 4 * 2 * SHARD
GROUP = 4


def sort_tiles(z, core, src, row, col):
    delta = jnp.bitwise_and(src // 2 - z + RING, RING - 1)
    slot = jnp.where(delta <= 3, 2 * delta, 2 * (RING - delta) - 1)
    slot = jnp.where(delta == 4, 7, slot)
    own = src % 2 == core
    early = jnp.logical_or(slot < 5, jnp.logical_and(own, slot < 7))
    first = jnp.where(own, jnp.where(slot < 5, slot, slot + 5), slot + 5)
    second = jnp.where(slot == 7, jnp.where(own, 2, 3), slot - 5)
    key = jnp.where(early, 0, ROWS) + row
    ids = jnp.arange(TILES, dtype=jnp.int32)
    record = ids * 128 + jnp.where(early, first, second) * COLS + col
    rank = key * TILES + ids
    spot = jnp.sum((rank[None, :] < rank[:, None]).astype(jnp.int32), axis=1)
    meta = jnp.sum(jnp.where(spot[None, :] == ids[:, None], record[None, :], 0), axis=1)
    marks = jnp.arange(16, dtype=jnp.int32)
    starts = jnp.sum((key[None, :] < marks[:, None]).astype(jnp.int32), axis=1)
    return meta, jnp.where(marks == 15, core, starts)


def row_sum(run, meta_ref, starts_ref, w_ref, fbuf, begin):
    lo = starts_ref[run]
    hi = starts_ref[run + 1]

    def step(k, total):
        weights = []
        sources = []
        for j in range(GROUP):
            at = lo + GROUP * k + j
            record = meta_ref[jnp.minimum(at, hi - 1)]
            tile = w_ref[jnp.right_shift(record, 7)]
            weights.append(jnp.where(at < hi, tile, jnp.zeros_like(tile)))
            sources.append(fbuf[jnp.bitwise_and(record, 127)])
        for j in range(0, GROUP, 2):
            total = total + jnp.dot(
                jnp.concatenate(weights[j : j + 2], axis=1),
                jnp.concatenate(sources[j : j + 2], axis=0),
                preferred_element_type=jnp.float32,
            )
        return total

    return lax.fori_loop(0, (hi - lo + GROUP - 1) // GROUP, step, begin)


def first_kernel(meta_ref, starts_ref, w_ref, own_hbm, other_hbm, next_hbm, out_ref, fbuf, fsem):
    moves = [
        pltpu.make_async_copy(own_hbm, fbuf.at[pl.ds(0, 5 * COLS)], fsem.at[0]),
        pltpu.make_async_copy(other_hbm, fbuf.at[pl.ds(5 * COLS, 5 * COLS)], fsem.at[1]),
        pltpu.make_async_copy(
            next_hbm.at[pl.ds(0, 2 * COLS)], fbuf.at[pl.ds(10 * COLS, 2 * COLS)], fsem.at[2]
        ),
    ]
    for move in moves:
        move.start()
    for move in moves:
        move.wait()
    for r in range(ROWS):
        begin = jnp.zeros((TILE, FEATURES), jnp.float32)
        out_ref[r] = row_sum(r, meta_ref, starts_ref, w_ref, fbuf, begin)


def normed(values, gain):
    mean_square = jnp.mean(values * values, axis=-1, keepdims=True)
    return (values * lax.rsqrt(mean_square + 1e-06) * gain).astype(jnp.bfloat16)


def last_kernel(
    meta_ref,
    starts_ref,
    w_ref,
    tiles_hbm,
    own_hbm,
    other_hbm,
    late_hbm,
    late_other_hbm,
    up_hbm,
    down_hbm,
    gain_one_ref,
    gain_two_ref,
    in_ref,
    out_ref,
    fbuf,
    up_ref,
    down_ref,
    own_ref,
    other_ref,
    shard_ref,
    rows_ref,
    acc_ref,
    fsem,
    wsem,
):
    blocks = [
        pltpu.make_async_copy(tiles_hbm.at[pl.ds(0, 2 * COLS)], fbuf.at[pl.ds(0, 2 * COLS)], fsem.at[0]),
        pltpu.make_async_copy(late_hbm, fbuf.at[pl.ds(2 * COLS, COLS)], fsem.at[1]),
        pltpu.make_async_copy(late_other_hbm, fbuf.at[pl.ds(3 * COLS, COLS)], fsem.at[2]),
    ]
    layers = [
        pltpu.make_async_copy(up_hbm.at[:, pl.ds(h * 256, 256)], up_ref.at[h], wsem.at[h])
        for h in range(4)
    ] + [
        pltpu.make_async_copy(down_hbm, down_ref, wsem.at[4]),
        pltpu.make_async_copy(own_hbm.at[pl.ds(2 * SRC, PACK)], own_ref, wsem.at[5]),
        pltpu.make_async_copy(other_hbm.at[pl.ds(2 * SRC, PACK)], other_ref, wsem.at[6]),
    ]
    for move in blocks + layers:
        move.start()
    for move in blocks:
        move.wait()
    for r in range(ROWS):
        acc_ref[pl.ds(r * TILE, TILE)] = row_sum(
            ROWS + r, meta_ref, starts_ref, w_ref, fbuf, in_ref[r]
        )
    for move in layers:
        move.wait()
    low = starts_ref[15] == 0
    for q in range(4):
        base = 2 * SHARD * q
        for k, at in ((0, 0), (3, HALF + SHARD)):
            mine = own_ref[base + at : base + at + HALF]
            theirs = other_ref[base + at : base + at + HALF]
            shard_ref[4 * q + k, :HALF] = jnp.where(low, mine, theirs)
            shard_ref[4 * q + k, HALF:] = jnp.where(low, theirs, mine)
        shard_ref[4 * q + 1] = own_ref[base + HALF : base + HALF + SHARD]
        shard_ref[4 * q + 2] = other_ref[base + HALF : base + HALF + SHARD]

    block = 256
    spans = [pl.ds(m * block, block) for m in range(DEST // block)]
    for at in spans:
        rows_ref[at] = normed(acc_ref[at], gain_one_ref[...])

    def layer_one(h, carry):
        for at in spans:
            hidden = jnp.dot(rows_ref[at], up_ref[h], preferred_element_type=jnp.float32)
            hidden = jnp.maximum(hidden, 0.0).astype(jnp.bfloat16)
            acc_ref[at] += jnp.dot(hidden, down_ref[h], preferred_element_type=jnp.float32)
        return carry

    lax.fori_loop(0, HIDDEN_ONE // block, layer_one, 0)
    for at in spans:
        rows_ref[at] = normed(acc_ref[at], gain_two_ref[...])

    def layer_two(pair, carry):
        left = shard_ref[2 * pair]
        right = shard_ref[2 * pair + 1]
        below = jnp.concatenate([left[FEATURES:], right[FEATURES:]], axis=0)
        for at in spans:
            parts = []
            for piece in (left, right):
                both = jnp.dot(rows_ref[at], piece[:FEATURES], preferred_element_type=jnp.float32)
                gate = both[:, :TILE]
                parts.append((gate * jax.nn.sigmoid(gate) * both[:, TILE:]).astype(jnp.bfloat16))
            acc_ref[at] += jnp.dot(
                jnp.concatenate(parts, axis=1), below, preferred_element_type=jnp.float32
            )
        return carry

    lax.fori_loop(0, 8, layer_two, 0)
    for at in spans:
        out_ref[at] = acc_ref[at].astype(jnp.bfloat16)


SMEM = pl.BlockSpec(memory_space=pltpu.SMEM)
HBM = pl.BlockSpec(memory_space=pltpu.HBM)
VMEM = pl.BlockSpec(memory_space=pltpu.VMEM)
SUMS = jax.ShapeDtypeStruct((ROWS, TILE, FEATURES), jnp.float32)
PARAMS = pltpu.CompilerParams(vmem_limit_bytes=40 << 20)


def first_sums(meta, starts, masked, own, other, following):
    return pl.pallas_call(
        first_kernel,
        out_shape=SUMS,
        in_specs=[SMEM, SMEM, VMEM, HBM, HBM, HBM],
        out_specs=VMEM,
        scratch_shapes=[
            pltpu.VMEM((12 * COLS, TILE, FEATURES), jnp.bfloat16),
            pltpu.SemaphoreType.DMA((3,)),
        ],
        compiler_params=PARAMS,
        name="first_sums",
    )(meta, starts, masked, own, other, following)


def last_stage(meta, starts, masked, blocks, own, other, late, late_other, up_one, down_one, gain_one, gain_two, sums):
    return pl.pallas_call(
        last_kernel,
        out_shape=jax.ShapeDtypeStruct((DEST, FEATURES), jnp.bfloat16),
        in_specs=[SMEM, SMEM, VMEM] + [HBM] * 7 + [VMEM] * 3,
        out_specs=VMEM,
        scratch_shapes=[
            pltpu.VMEM((4 * COLS, TILE, FEATURES), jnp.bfloat16),
            pltpu.VMEM((4, FEATURES, HIDDEN_ONE // 4), jnp.bfloat16),
            pltpu.VMEM((4, HIDDEN_ONE // 4, FEATURES), jnp.bfloat16),
            pltpu.VMEM((PACK, FEATURES), jnp.bfloat16),
            pltpu.VMEM((PACK, FEATURES), jnp.bfloat16),
            pltpu.VMEM((16, SHARD, FEATURES), jnp.bfloat16),
            pltpu.VMEM((DEST, FEATURES), jnp.bfloat16),
            pltpu.VMEM((DEST, FEATURES), jnp.float32),
            pltpu.SemaphoreType.DMA((3,)),
            pltpu.SemaphoreType.DMA((7,)),
        ],
        compiler_params=PARAMS,
        name="last_stage",
    )(meta, starts, masked, blocks, own, other, late, late_other, up_one, down_one, gain_one, gain_two, sums)


UP = [(i, (i + 1) % RING) for i in range(RING)]
DOWN = [(i, (i - 1) % RING) for i in range(RING)]
SWAP = [(0, 1), (1, 0)]
X_SPLIT = [(x, (x + 1) % 4) for x in range(4)] + [(4 + x, 4 + (x - 1) % 4) for x in range(4)]
X_FAR = [(x, (x + 2) % 4) for x in range(4)]
Y_UP = [(i, (i + 1) % 4) for i in range(4)]
Y_DOWN = [(i, (i - 1) % 4) for i in range(4)]
Y_SPLIT = Y_UP + [(4 + i, 4 + (i - 1) % 4) for i in range(4)]
Y = ("yhi", "ylo")


def local(
    features,
    tile_weight,
    tile_limit,
    tile_src,
    tile_row,
    tile_col,
    gain_one,
    up_one,
    down_one,
    gain_two,
    gate_two,
    up_two,
    down_two,
):
    core = lax.axis_index("core").astype(jnp.int32)
    z = lax.axis_index("z").astype(jnp.int32)
    shard = jnp.concatenate([jnp.concatenate([gate_two, up_two], axis=1), down_two.T], axis=0)
    part = lax.dynamic_slice_in_dim(shard, core * HALF, HALF, 0)

    up1 = lax.ppermute(features, "z", UP)
    dn1 = lax.ppermute(features, "z", DOWN)
    side = lax.ppermute(shard, ("core", "x"), X_SPLIT)
    far = lax.ppermute(part, "x", X_FAR)
    columns = jnp.arange(TILE, dtype=jnp.int32)
    masked = jnp.where(
        columns[None, None, :] < tile_limit[:, :, None],
        tile_weight,
        jnp.zeros((), tile_weight.dtype),
    )
    up1, dn1, side, far, masked = lax.optimization_barrier((up1, dn1, side, far, masked))

    up2 = lax.ppermute(up1, "z", UP)
    dn2 = lax.ppermute(dn1, "z", DOWN)
    pack = jnp.concatenate([part, side, far], axis=0)
    pack1 = lax.ppermute(pack, Y, Y_UP)
    pack3 = lax.ppermute(pack, Y, Y_DOWN)
    meta, starts = sort_tiles(z, core, tile_src[:, 0], tile_row, tile_col)
    up2, dn2, pack1, pack3, meta, starts = lax.optimization_barrier((up2, dn2, pack1, pack3, meta, starts))

    up3 = lax.ppermute(up2, "z", UP)
    dn3 = lax.ppermute(dn2, "z", DOWN)
    pack2 = lax.ppermute(jnp.where(core == 0, pack1, pack3), ("core",) + Y, Y_SPLIT)
    own = jnp.concatenate([features, up1, dn1, up2, dn2], axis=0)
    other = lax.ppermute(own, "core", SWAP)
    up3, dn3, pack2, own, other = lax.optimization_barrier((up3, dn3, pack2, own, other))

    up4 = lax.ppermute(up3[: SRC // 2], "z", UP)
    dn4 = lax.ppermute(dn3[SRC // 2 :], "z", DOWN)
    own_next = jnp.concatenate([up3, dn3, pack, pack1, pack2, pack3], axis=0)
    other_next = lax.ppermute(own_next, "core", SWAP)
    late = jnp.concatenate([up4, dn4], axis=0)
    late_other = lax.ppermute(late, "core", SWAP)

    tiles = lambda a: a.reshape(-1, TILE, FEATURES)
    sums = first_sums(meta, starts, masked, tiles(own), tiles(other), tiles(own_next))
    return last_stage(
        meta,
        starts,
        masked,
        tiles(other_next),
        own_next,
        other_next,
        tiles(late),
        tiles(late_other),
        up_one,
        down_one.reshape(4, HIDDEN_ONE // 4, FEATURES),
        gain_one[None, :],
        gain_two[None, :],
        sums,
    )


def solution(mesh):
    fine = Mesh(mesh.devices.reshape(8, 2, 2, 4, 2), ("z", "core", "yhi", "x", "ylo"))
    every = ("z", "core", "yhi", "x", "ylo")
    plane = ("yhi", "x", "ylo")
    in_specs = (
        P(("z", "core"), None),
        P(every, None, None),
        P(every, None),
        P(every, None),
        P(every),
        P(every),
        P(),
        P(),
        P(),
        P(),
        P(None, plane),
        P(None, plane),
        P(None, plane),
    )
    return jax.shard_map(local, mesh=fine, in_specs=in_specs, out_specs=P(every, None), check_vma=False)
```

```python
import jax
import jax.numpy as jnp
from jax import lax
from jax.experimental import pallas as pl
from jax.experimental.pallas import tpu as pltpu
from jax.sharding import Mesh, PartitionSpec as P


FEATURES = 256
TILE = 128
SRC = 1024
DEST = 768
TILES = 192
ROWS = DEST // TILE
COLS = SRC // TILE
HIDDEN_ONE = 1024
SHARD = 384
HALF = SHARD // 2
RING = 8
GROUP = 4


def sort_tiles(z, core, src, row, col):
    delta = jnp.bitwise_and(src // 2 - z + RING, RING - 1)
    slot = jnp.where(delta <= 3, 2 * delta, 2 * (RING - delta) - 1)
    slot = jnp.where(delta == 4, 7, slot)
    own = src % 2 == core
    theirs = jnp.where(slot < 5, 1, 3)
    group = jnp.where(own, jnp.where(slot < 5, 0, jnp.where(slot < 7, 2, 3)), theirs)
    final = jnp.where(slot == 7, jnp.where(own, 2, 3), slot - 5)
    at = jnp.where(slot < 5, slot, jnp.where(group == 2, slot - 5, final))
    key = group * ROWS + row
    ids = jnp.arange(TILES, dtype=jnp.int32)
    record = ids * 128 + at * COLS + col
    rank = key * TILES + ids
    spot = jnp.sum((rank[None, :] < rank[:, None]).astype(jnp.int32), axis=1)
    meta = jnp.sum(jnp.where(spot[None, :] == ids[:, None], record[None, :], 0), axis=1)
    marks = jnp.arange(32, dtype=jnp.int32)
    starts = jnp.sum((key[None, :] < marks[:, None]).astype(jnp.int32), axis=1)
    return meta, jnp.where(marks == 31, core, starts)


def row_sum(run, meta_ref, starts_ref, w_ref, rest_ref, fbuf, begin):
    lo = starts_ref[run]
    hi = starts_ref[run + 1]

    def step(k, total):
        weights = []
        sources = []
        for j in range(GROUP):
            at = lo + GROUP * k + j
            record = meta_ref[jnp.minimum(at, hi - 1)]
            number = jnp.right_shift(record, 7)
            tile = jnp.where(
                number < TILES // 2,
                w_ref[jnp.minimum(number, TILES // 2 - 1)],
                rest_ref[jnp.maximum(number - TILES // 2, 0)],
            )
            weights.append(jnp.where(at < hi, tile, jnp.zeros_like(tile)))
            sources.append(fbuf[jnp.bitwise_and(record, 127)])
        for j in range(0, GROUP, 2):
            total = total + jnp.dot(
                jnp.concatenate(weights[j : j + 2], axis=1),
                jnp.concatenate(sources[j : j + 2], axis=0),
                preferred_element_type=jnp.float32,
            )
        return total

    return lax.fori_loop(0, (hi - lo + GROUP - 1) // GROUP, step, begin)


def first_kernel(meta_ref, starts_ref, w_ref, rest_ref, own_ref, out_ref):
    for r in range(ROWS):
        begin = jnp.zeros((TILE, FEATURES), jnp.float32)
        out_ref[r] = row_sum(r, meta_ref, starts_ref, w_ref, rest_ref, own_ref, begin)


def second_kernel(meta_ref, starts_ref, w_ref, rest_ref, other_ref, next_ref, in_ref, out_ref):
    for r in range(ROWS):
        held = row_sum(ROWS + r, meta_ref, starts_ref, w_ref, rest_ref, other_ref, in_ref[r])
        out_ref[r] = row_sum(2 * ROWS + r, meta_ref, starts_ref, w_ref, rest_ref, next_ref, held)


def normed(values, gain):
    mean_square = jnp.mean(values * values, axis=-1, keepdims=True)
    return (values * lax.rsqrt(mean_square + 1e-06) * gain).astype(jnp.bfloat16)


def last_kernel(
    meta_ref,
    starts_ref,
    w_ref,
    rest_ref,
    tiles_ref,
    own_ref,
    other_ref,
    late_ref,
    late_other_ref,
    up_ref,
    down_ref,
    gain_one_ref,
    gain_two_ref,
    in_ref,
    out_ref,
    fbuf,
    shard_ref,
    rows_ref,
    acc_ref,
):
    fbuf[: 2 * COLS] = tiles_ref[: 2 * COLS]
    fbuf[2 * COLS : 3 * COLS] = late_ref[...]
    fbuf[3 * COLS :] = late_other_ref[...]
    for r in range(ROWS):
        acc_ref[pl.ds(r * TILE, TILE)] = row_sum(
            3 * ROWS + r, meta_ref, starts_ref, w_ref, rest_ref, fbuf, in_ref[r]
        )
    low = starts_ref[31] == 0
    for q in range(4):
        base = 2 * SRC + 2 * SHARD * q
        for k, at in ((0, 0), (3, HALF + SHARD)):
            mine = own_ref[base + at : base + at + HALF]
            theirs = other_ref[base + at : base + at + HALF]
            shard_ref[4 * q + k, :HALF] = jnp.where(low, mine, theirs)
            shard_ref[4 * q + k, HALF:] = jnp.where(low, theirs, mine)
        shard_ref[4 * q + 1] = own_ref[base + HALF : base + HALF + SHARD]
        shard_ref[4 * q + 2] = other_ref[base + HALF : base + HALF + SHARD]

    block = 256
    spans = [pl.ds(m * block, block) for m in range(DEST // block)]
    for at in spans:
        rows_ref[at] = normed(acc_ref[at], gain_one_ref[...])

    for h in range(HIDDEN_ONE // block):
        for at in spans:
            hidden = jnp.dot(
                rows_ref[at],
                up_ref[:, h * block : (h + 1) * block],
                preferred_element_type=jnp.float32,
            )
            hidden = jnp.maximum(hidden, 0.0).astype(jnp.bfloat16)
            acc_ref[at] += jnp.dot(
                hidden, down_ref[h * block : (h + 1) * block], preferred_element_type=jnp.float32
            )
    for at in spans:
        rows_ref[at] = normed(acc_ref[at], gain_two_ref[...])

    wide = [pl.ds(m * 384, 384) for m in range(2)]

    def layer_two(pair, carry):
        left = shard_ref[2 * pair]
        right = shard_ref[2 * pair + 1]
        below = jnp.concatenate([left[FEATURES:], right[FEATURES:]], axis=0)
        for at in wide:
            parts = []
            for piece in (left, right):
                both = jnp.dot(rows_ref[at], piece[:FEATURES], preferred_element_type=jnp.float32)
                gate = 0.5 * both[:, :TILE]
                parts.append(((gate + gate * jnp.tanh(gate)) * both[:, TILE:]).astype(jnp.bfloat16))
            acc_ref[at] += jnp.dot(
                jnp.concatenate(parts, axis=1), below, preferred_element_type=jnp.float32
            )
        return carry

    lax.fori_loop(0, 8, layer_two, 0)
    for at in spans:
        out_ref[at] = acc_ref[at].astype(jnp.bfloat16)


SMEM = pl.BlockSpec(memory_space=pltpu.SMEM)
VMEM = pl.BlockSpec(memory_space=pltpu.VMEM)
SUMS = jax.ShapeDtypeStruct((ROWS, TILE, FEATURES), jnp.float32)


def part_sums(kernel, *operands):
    return pl.pallas_call(
        kernel,
        out_shape=SUMS,
        in_specs=[SMEM, SMEM] + [VMEM] * (len(operands) - 2),
        out_specs=VMEM,
        compiler_params=pltpu.CompilerParams(vmem_limit_bytes=4 << 20),
    )(*operands)


def last_stage(*operands):
    return pl.pallas_call(
        last_kernel,
        out_shape=jax.ShapeDtypeStruct((DEST, FEATURES), jnp.bfloat16),
        in_specs=[SMEM, SMEM] + [VMEM] * (len(operands) - 2),
        out_specs=VMEM,
        scratch_shapes=[
            pltpu.VMEM((4 * COLS, TILE, FEATURES), jnp.bfloat16),
            pltpu.VMEM((16, SHARD, FEATURES), jnp.bfloat16),
            pltpu.VMEM((DEST, FEATURES), jnp.bfloat16),
            pltpu.VMEM((DEST, FEATURES), jnp.float32),
        ],
        compiler_params=pltpu.CompilerParams(vmem_limit_bytes=14 << 20),
        name="last_stage",
    )(*operands)


UP = [(i, (i + 1) % RING) for i in range(RING)]
DOWN = [(i, (i - 1) % RING) for i in range(RING)]
SWAP = [(0, 1), (1, 0)]
X_SPLIT = [(x, (x + 1) % 4) for x in range(4)] + [(4 + x, 4 + (x - 1) % 4) for x in range(4)]
X_FAR = [(x, (x + 2) % 4) for x in range(4)]
Y_UP = [(i, (i + 1) % 4) for i in range(4)]
Y_DOWN = [(i, (i - 1) % 4) for i in range(4)]
Y_SPLIT = Y_UP + [(4 + i, 4 + (i - 1) % 4) for i in range(4)]
Y = ("yhi", "ylo")


def local(
    features,
    tile_weight,
    tile_limit,
    tile_src,
    tile_row,
    tile_col,
    gain_one,
    up_one,
    down_one,
    gain_two,
    gate_two,
    up_two,
    down_two,
):
    core = lax.axis_index("core").astype(jnp.int32)
    z = lax.axis_index("z").astype(jnp.int32)
    shard = jnp.concatenate([jnp.concatenate([gate_two, up_two], axis=1), down_two.T], axis=0)
    part = lax.dynamic_slice_in_dim(shard, core * HALF, HALF, 0)

    up1 = lax.ppermute(features, "z", UP)
    dn1 = lax.ppermute(features, "z", DOWN)
    side = lax.ppermute(shard, ("core", "x"), X_SPLIT)
    far = lax.ppermute(part, "x", X_FAR)
    columns = jnp.arange(TILE, dtype=jnp.int32)

    def keep(begin, limits):
        weight = tile_weight[begin : begin + TILES // 2]
        limit = limits[begin : begin + TILES // 2]
        return jnp.where(
            columns[None, None, :] < limit[:, :, None], weight, jnp.zeros((), weight.dtype)
        )

    masked = keep(0, tile_limit)
    up1, dn1, side, far, masked, limits = lax.optimization_barrier(
        (up1, dn1, side, far, masked, tile_limit)
    )
    masked_rest = keep(TILES // 2, limits)

    up2 = lax.ppermute(up1, "z", UP)
    dn2 = lax.ppermute(dn1, "z", DOWN)
    pack = jnp.concatenate([part, side, far], axis=0)
    pack1 = lax.ppermute(pack, Y, Y_UP)
    pack3 = lax.ppermute(pack, Y, Y_DOWN)
    meta, starts = sort_tiles(z, core, tile_src[:, 0], tile_row, tile_col)
    up2, dn2, pack1, pack3, meta, starts, masked_rest = lax.optimization_barrier(
        (up2, dn2, pack1, pack3, meta, starts, masked_rest)
    )

    up3 = lax.ppermute(up2, "z", UP)
    dn3 = lax.ppermute(dn2, "z", DOWN)
    pack2 = lax.ppermute(jnp.where(core == 0, pack1, pack3), ("core",) + Y, Y_SPLIT)
    own = jnp.concatenate([features, up1, dn1, up2, dn2], axis=0)
    other = lax.ppermute(own, "core", SWAP)
    tiles = lambda a: a.reshape(-1, TILE, FEATURES)
    sums = part_sums(first_kernel, meta, starts, masked, masked_rest, tiles(own))
    up3, dn3, pack2, other, sums = lax.optimization_barrier((up3, dn3, pack2, other, sums))

    up4 = lax.ppermute(up3[: SRC // 2], "z", UP)
    dn4 = lax.ppermute(dn3[SRC // 2 :], "z", DOWN)
    own_next = jnp.concatenate([up3, dn3, pack, pack1, pack2, pack3], axis=0)
    other_next = lax.ppermute(own_next, "core", SWAP)
    late = jnp.concatenate([up4, dn4], axis=0)
    late_other = lax.ppermute(late, "core", SWAP)
    sums = part_sums(
        second_kernel, meta, starts, masked, masked_rest, tiles(other), tiles(own_next), sums
    )
    return last_stage(
        meta,
        starts,
        masked,
        masked_rest,
        tiles(other_next),
        own_next,
        other_next,
        tiles(late),
        tiles(late_other),
        up_one,
        down_one,
        gain_one[None, :],
        gain_two[None, :],
        sums,
    )


def solution(mesh):
    fine = Mesh(mesh.devices.reshape(8, 2, 2, 4, 2), ("z", "core", "yhi", "x", "ylo"))
    every = ("z", "core", "yhi", "x", "ylo")
    plane = ("yhi", "x", "ylo")
    in_specs = (
        P(("z", "core"), None),
        P(every, None, None),
        P(every, None),
        P(every, None),
        P(every),
        P(every),
        P(),
        P(),
        P(),
        P(),
        P(None, plane),
        P(None, plane),
        P(None, plane),
    )
    return jax.shard_map(local, mesh=fine, in_specs=in_specs, out_specs=P(every, None), check_vma=False)
```

```python
import jax
import jax.numpy as jnp
from jax import lax
from jax.experimental import pallas as pl
from jax.experimental.pallas import tpu as pltpu
from jax.sharding import Mesh, PartitionSpec as P


FEATURES = 256
TILE = 128
SRC = 1024
DEST = 768
TILES = 192
ROWS = DEST // TILE
COLS = SRC // TILE
HIDDEN_ONE = 1024
SHARD = 384
HALF = SHARD // 2
RING = 8
GROUP = 4


def sort_tiles(z, core, src, row, col):
    delta = jnp.bitwise_and(src // 2 - z + RING, RING - 1)
    slot = jnp.where(delta <= 3, 2 * delta, 2 * (RING - delta) - 1)
    slot = jnp.where(delta == 4, 7, slot)
    own = src % 2 == core
    theirs = jnp.where(slot < 5, 1, 3)
    group = jnp.where(own, jnp.where(slot < 5, 0, jnp.where(slot < 7, 2, 3)), theirs)
    final = jnp.where(slot == 7, jnp.where(own, 2, 3), slot - 5)
    at = jnp.where(slot < 5, slot, jnp.where(group == 2, slot - 5, final))
    key = group * ROWS + row
    ids = jnp.arange(TILES, dtype=jnp.int32)
    record = ids * 128 + at * COLS + col
    rank = key * TILES + ids
    spot = jnp.sum((rank[None, :] < rank[:, None]).astype(jnp.int32), axis=1)
    meta = jnp.sum(jnp.where(spot[None, :] == ids[:, None], record[None, :], 0), axis=1)
    marks = jnp.arange(32, dtype=jnp.int32)
    starts = jnp.sum((key[None, :] < marks[:, None]).astype(jnp.int32), axis=1)
    return meta, jnp.where(marks == 31, core, starts)


def row_sum(run, meta_ref, starts_ref, w_ref, fbuf, begin):
    lo = starts_ref[run]
    hi = starts_ref[run + 1]

    def step(k, total):
        weights = []
        sources = []
        for j in range(GROUP):
            at = lo + GROUP * k + j
            record = meta_ref[jnp.minimum(at, hi - 1)]
            tile = w_ref[jnp.right_shift(record, 7)]
            weights.append(jnp.where(at < hi, tile, jnp.zeros_like(tile)))
            sources.append(fbuf[jnp.bitwise_and(record, 127)])
        for j in range(0, GROUP, 2):
            total = total + jnp.dot(
                jnp.concatenate(weights[j : j + 2], axis=1),
                jnp.concatenate(sources[j : j + 2], axis=0),
                preferred_element_type=jnp.float32,
            )
        return total

    return lax.fori_loop(0, (hi - lo + GROUP - 1) // GROUP, step, begin)


def first_kernel(meta_ref, starts_ref, w_ref, own_ref, out_ref):
    for r in range(ROWS):
        begin = jnp.zeros((TILE, FEATURES), jnp.float32)
        out_ref[r] = row_sum(r, meta_ref, starts_ref, w_ref, own_ref, begin)


def second_kernel(meta_ref, starts_ref, w_ref, other_ref, next_ref, in_ref, out_ref):
    for r in range(ROWS):
        held = row_sum(ROWS + r, meta_ref, starts_ref, w_ref, other_ref, in_ref[r])
        out_ref[r] = row_sum(2 * ROWS + r, meta_ref, starts_ref, w_ref, next_ref, held)


def normed(values, gain):
    mean_square = jnp.mean(values * values, axis=-1, keepdims=True)
    return (values * lax.rsqrt(mean_square + 1e-06) * gain).astype(jnp.bfloat16)


def last_kernel(
    meta_ref,
    starts_ref,
    w_ref,
    tiles_ref,
    own_ref,
    other_ref,
    late_ref,
    late_other_ref,
    up_ref,
    down_ref,
    gain_one_ref,
    gain_two_ref,
    in_ref,
    out_ref,
    fbuf,
    shard_ref,
    rows_ref,
    acc_ref,
):
    fbuf[: 2 * COLS] = tiles_ref[: 2 * COLS]
    fbuf[2 * COLS : 3 * COLS] = late_ref[...]
    fbuf[3 * COLS :] = late_other_ref[...]
    for r in range(ROWS):
        acc_ref[pl.ds(r * TILE, TILE)] = row_sum(
            3 * ROWS + r, meta_ref, starts_ref, w_ref, fbuf, in_ref[r]
        )
    low = starts_ref[31] == 0
    for q in range(4):
        base = 2 * SRC + 2 * SHARD * q
        for k, at in ((0, 0), (3, HALF + SHARD)):
            mine = own_ref[base + at : base + at + HALF]
            theirs = other_ref[base + at : base + at + HALF]
            shard_ref[4 * q + k, :HALF] = jnp.where(low, mine, theirs)
            shard_ref[4 * q + k, HALF:] = jnp.where(low, theirs, mine)
        shard_ref[4 * q + 1] = own_ref[base + HALF : base + HALF + SHARD]
        shard_ref[4 * q + 2] = other_ref[base + HALF : base + HALF + SHARD]

    block = 256
    spans = [pl.ds(m * block, block) for m in range(DEST // block)]
    for at in spans:
        rows_ref[at] = normed(acc_ref[at], gain_one_ref[...])

    for h in range(HIDDEN_ONE // block):
        for at in spans:
            hidden = jnp.dot(
                rows_ref[at],
                up_ref[:, h * block : (h + 1) * block],
                preferred_element_type=jnp.float32,
            )
            hidden = jnp.maximum(hidden, 0.0).astype(jnp.bfloat16)
            acc_ref[at] += jnp.dot(
                hidden, down_ref[h * block : (h + 1) * block], preferred_element_type=jnp.float32
            )
    for at in spans:
        rows_ref[at] = normed(acc_ref[at], gain_two_ref[...])

    wide = [pl.ds(m * 384, 384) for m in range(DEST // 384)]

    def layer_two(pair, carry):
        left = shard_ref[2 * pair]
        right = shard_ref[2 * pair + 1]
        below = jnp.concatenate([left[FEATURES:], right[FEATURES:]], axis=0)
        for at in wide:
            parts = []
            for piece in (left, right):
                both = jnp.dot(rows_ref[at], piece[:FEATURES], preferred_element_type=jnp.float32)
                gate = 0.5 * both[:, :TILE]
                parts.append(((gate + gate * jnp.tanh(gate)) * both[:, TILE:]).astype(jnp.bfloat16))
            acc_ref[at] += jnp.dot(
                jnp.concatenate(parts, axis=1), below, preferred_element_type=jnp.float32
            )
        return carry

    lax.fori_loop(0, 8, layer_two, 0)
    for at in spans:
        out_ref[at] = acc_ref[at].astype(jnp.bfloat16)


SMEM = pl.BlockSpec(memory_space=pltpu.SMEM)
VMEM = pl.BlockSpec(memory_space=pltpu.VMEM)
SUMS = jax.ShapeDtypeStruct((ROWS, TILE, FEATURES), jnp.float32)


def part_sums(kernel, *operands):
    return pl.pallas_call(
        kernel,
        out_shape=SUMS,
        in_specs=[SMEM, SMEM] + [VMEM] * (len(operands) - 2),
        out_specs=VMEM,
        compiler_params=pltpu.CompilerParams(vmem_limit_bytes=4 << 20),
    )(*operands)


def last_stage(*operands):
    return pl.pallas_call(
        last_kernel,
        out_shape=jax.ShapeDtypeStruct((DEST, FEATURES), jnp.bfloat16),
        in_specs=[SMEM, SMEM] + [VMEM] * (len(operands) - 2),
        out_specs=VMEM,
        scratch_shapes=[
            pltpu.VMEM((4 * COLS, TILE, FEATURES), jnp.bfloat16),
            pltpu.VMEM((16, SHARD, FEATURES), jnp.bfloat16),
            pltpu.VMEM((DEST, FEATURES), jnp.bfloat16),
            pltpu.VMEM((DEST, FEATURES), jnp.float32),
        ],
        compiler_params=pltpu.CompilerParams(vmem_limit_bytes=14 << 20),
        name="last_stage",
    )(*operands)


UP = [(i, (i + 1) % RING) for i in range(RING)]
DOWN = [(i, (i - 1) % RING) for i in range(RING)]
SWAP = [(0, 1), (1, 0)]
X_SPLIT = [(x, (x + 1) % 4) for x in range(4)] + [(4 + x, 4 + (x - 1) % 4) for x in range(4)]
X_FAR = [(x, (x + 2) % 4) for x in range(4)]
Y_UP = [(i, (i + 1) % 4) for i in range(4)]
Y_DOWN = [(i, (i - 1) % 4) for i in range(4)]
Y_SPLIT = Y_UP + [(4 + i, 4 + (i - 1) % 4) for i in range(4)]
Y = ("yhi", "ylo")


def local(
    features,
    tile_weight,
    tile_limit,
    tile_src,
    tile_row,
    tile_col,
    gain_one,
    up_one,
    down_one,
    gain_two,
    gate_two,
    up_two,
    down_two,
):
    core = lax.axis_index("core").astype(jnp.int32)
    z = lax.axis_index("z").astype(jnp.int32)
    shard = jnp.concatenate([jnp.concatenate([gate_two, up_two], axis=1), down_two.T], axis=0)
    part = lax.dynamic_slice_in_dim(shard, core * HALF, HALF, 0)

    up1 = lax.ppermute(features, "z", UP)
    dn1 = lax.ppermute(features, "z", DOWN)
    side = lax.ppermute(shard, ("core", "x"), X_SPLIT)
    far = lax.ppermute(part, "x", X_FAR)
    columns = jnp.arange(TILE, dtype=jnp.int32)
    masked = jnp.where(
        columns[None, None, :] < tile_limit[:, :, None],
        tile_weight,
        jnp.zeros((), tile_weight.dtype),
    )
    up1, dn1, side, far, masked = lax.optimization_barrier((up1, dn1, side, far, masked))

    up2 = lax.ppermute(up1, "z", UP)
    dn2 = lax.ppermute(dn1, "z", DOWN)
    pack = jnp.concatenate([part, side, far], axis=0)
    pack1 = lax.ppermute(pack, Y, Y_UP)
    pack3 = lax.ppermute(pack, Y, Y_DOWN)
    meta, starts = sort_tiles(z, core, tile_src[:, 0], tile_row, tile_col)
    up2, dn2, pack1, pack3, meta, starts = lax.optimization_barrier((up2, dn2, pack1, pack3, meta, starts))

    up3 = lax.ppermute(up2, "z", UP)
    dn3 = lax.ppermute(dn2, "z", DOWN)
    pack2 = lax.ppermute(jnp.where(core == 0, pack1, pack3), ("core",) + Y, Y_SPLIT)
    own = jnp.concatenate([features, up1, dn1, up2, dn2], axis=0)
    other = lax.ppermute(own, "core", SWAP)
    tiles = lambda a: a.reshape(-1, TILE, FEATURES)
    sums = part_sums(first_kernel, meta, starts, masked, tiles(own))
    up3, dn3, pack2, other, sums = lax.optimization_barrier((up3, dn3, pack2, other, sums))

    up4 = lax.ppermute(up3[: SRC // 2], "z", UP)
    dn4 = lax.ppermute(dn3[SRC // 2 :], "z", DOWN)
    own_next = jnp.concatenate([up3, dn3, pack, pack1, pack2, pack3], axis=0)
    other_next = lax.ppermute(own_next, "core", SWAP)
    late = jnp.concatenate([up4, dn4], axis=0)
    late_other = lax.ppermute(late, "core", SWAP)
    sums = part_sums(second_kernel, meta, starts, masked, tiles(other), tiles(own_next), sums)
    return last_stage(
        meta,
        starts,
        masked,
        tiles(other_next),
        own_next,
        other_next,
        tiles(late),
        tiles(late_other),
        up_one,
        down_one,
        gain_one[None, :],
        gain_two[None, :],
        sums,
    )


def solution(mesh):
    fine = Mesh(mesh.devices.reshape(8, 2, 2, 4, 2), ("z", "core", "yhi", "x", "ylo"))
    every = ("z", "core", "yhi", "x", "ylo")
    plane = ("yhi", "x", "ylo")
    in_specs = (
        P(("z", "core"), None),
        P(every, None, None),
        P(every, None),
        P(every, None),
        P(every),
        P(every),
        P(),
        P(),
        P(),
        P(),
        P(None, plane),
        P(None, plane),
        P(None, plane),
    )
    return jax.shard_map(local, mesh=fine, in_specs=in_specs, out_specs=P(every, None), check_vma=False)
```
